32 devices in a mesh: grp: 2 (over y), img: 4 (over z), sub: 2 (over x), cls: 2 (over core).
Axes of the slice: x: 2, y: 2, z: 4, core: 2. Of those that a mesh axis runs over, the one named last changes fastest.
Arguments:
- images: bfloat16 [4096, 3072], P(('grp', 'img', 'sub', 'cls')), parts along dimension 0, may hold values from -10 to 10
- labels: int32 [4096], P(('grp', 'img', 'sub', 'cls')), parts along dimension 0, may hold values from 0 to 999
- seeds: int32 [128], replicated, may hold values from 0 to 46336
Outputs:
- rfactor: float32 [1024, 512], P('grp'), parts along dimension 0
- projections: float32 [1024, 1000], P('grp', 'cls'), parts along dimension 0
The draws below stay inside these ranges and needn't reach their ends.
There are 2 independent parts, one for each index of `grp`. The reference program is written for one: setup_inputs(seed, part) draws one part's arguments, and reference() takes and returns one part's arrays. A program takes and returns all parts, laid end to end along the dimension named above; an argument that names none is the same for every part. Nothing has to cross between parts.
All inputs are finite; a program needn't handle non-finite values.
Results may differ from the reference program's by a relative error of at most 0.0058.
Values sent between devices are 32-bit elements; how exact they have to be, the bound alone decides.
A program may use at most 128 MiB of HBM per device.

```python
import math
import jax
import jax.numpy as jnp
from jax import lax

FILTERS = 128
FEAT = 512
CLASSES = 1000
PIXELS = 3072
IMAGES = 2048


def draw_images(key, part):
    key_noise, key_scale, key_pattern, key_phase = jax.random.split(key, 4)
    rows = jnp.arange(IMAGES, dtype=jnp.float32)[:, None] / IMAGES
    phase = jax.random.uniform(key_phase, (), jnp.float32, 0.0, 6.283185)
    noise = jnp.clip(jax.random.normal(key_noise, (IMAGES, PIXELS), jnp.float32), -4.0, 4.0)
    scale = jnp.exp(jax.random.uniform(key_scale, (IMAGES, 1), jnp.float32, math.log(0.5), math.log(2.0)))
    pattern = jax.random.uniform(key_pattern, (1, PIXELS), jnp.float32, -1.0, 1.0)
    amplitude = 1.2 * jnp.sin(6.283185 * 3.0 * rows + phase)
    return (noise * scale + amplitude * pattern).astype(jnp.bfloat16)


def touch_ends(drawn, stream_key, least, top_value):
    index_at = [jax.random.randint(jax.random.fold_in(stream_key, axis), (), 0, length) for axis, length in enumerate(drawn.shape)]
    widest = drawn.shape.index(max(drawn.shape))
    neighbour = index_at[:widest] + [(index_at[widest] + 1) % drawn.shape[widest]] + index_at[widest + 1:]
    return drawn.at[tuple(index_at)].set(least).at[tuple(neighbour)].set(top_value)


def setup_inputs(seed: int = 0, part: int = 0) -> dict:
    keys = jax.random.split(jax.random.key(seed), 4)
    part_splits = jax.random.split(jax.random.fold_in(keys[3], part), 4)
    return {
        "images": draw_images(jax.random.fold_in(jax.random.fold_in(keys[3], part), 71), part),
        "labels": touch_ends(jax.random.randint(part_splits[1], (IMAGES,), 0, CLASSES), jax.random.fold_in(part_splits[1], 1), 0, CLASSES - 1).astype(jnp.int32),
        "seeds": touch_ends(jax.random.randint(keys[2], (FILTERS,), 0, 46337), jax.random.fold_in(keys[2], 1), 0, 46336).astype(jnp.int32),
    }


def make_filters(seeds):
    count = seeds.shape[0]
    index = lax.broadcasted_iota(jnp.int32, (count, 108), 1)
    first = (seeds[:, None] * 7919 + index * 104729) % 46337
    second = (first * first + seeds[:, None]) % 46337
    values = (second.astype(jnp.float32) / 46337.0 - 0.5) * math.sqrt(12.0 / 108.0)
    return values.reshape(count, 3, 6, 6).astype(jnp.bfloat16)

def features_of(block, filters):
    pictures = block.reshape(block.shape[0], 3, 32, 32)
    response = lax.conv_general_dilated(pictures, filters, (2, 2), 'VALID', dimension_numbers=('NCHW', 'OIHW', 'NCHW'), preferred_element_type=jnp.float32)
    active = jnp.maximum(response, 0.0)
    active = active.reshape(block.shape[0], filters.shape[0], 2, 7, 2, 7)
    pooled = lax.optimization_barrier(jnp.mean(active, axis=(3, 5)))
    return pooled.reshape(block.shape[0], filters.shape[0] * 4)

def reference(images, labels, seeds):
    filters = make_filters(seeds)
    count = images.shape[0]
    width = min(1024, count)
    blocks = count // width
    image_blocks = images.reshape(blocks, width, images.shape[1])
    label_blocks = labels.reshape(blocks, width)
    classes_row = jnp.arange(CLASSES, dtype=jnp.int32)

    def accumulate(carry, pair):
        gram, sums = carry
        block, marks = pair
        feats = features_of(block, filters)
        onehot = (marks[:, None] == classes_row[None, :]).astype(jnp.float32)
        gram = gram + lax.dot_general(feats.astype(jnp.float32), feats.astype(jnp.float32), (((0,), (0,)), ((), ())), precision=lax.Precision.HIGHEST, preferred_element_type=jnp.float32)
        sums = sums + lax.dot_general(feats.astype(jnp.float32), onehot.astype(jnp.float32), (((0,), (0,)), ((), ())), precision=lax.Precision.HIGHEST, preferred_element_type=jnp.float32)
        return ((gram, sums), None)
    start = (jnp.zeros((FEAT, FEAT), jnp.float32), jnp.zeros((FEAT, CLASSES), jnp.float32))
    (gram, sums), _ = lax.scan(accumulate, start, (image_blocks, label_blocks))
    gram = gram + 0.001 * count * jnp.eye(FEAT, dtype=jnp.float32)
    lower = jnp.linalg.cholesky(gram)
    projections = lax.linalg.triangular_solve(lower, sums, left_side=True, lower=True)
    return (lower.T, projections)
```

```python
import math

import jax
import jax.numpy as jnp
from jax import lax
from jax.experimental import pallas as pl
from jax.experimental.pallas import tpu as pltpu
from jax.sharding import PartitionSpec as P

CLASSES = 1000
RIDGE = 0.001
PANEL = 128
STRIP = 32
BAND = 128
GATHER_LIMIT = 16 * 1024 * 1024
HIGHEST = lax.Precision.HIGHEST
MESH = pl.DeviceIdType.MESH


def pieces(value):
    first = value.astype(jnp.bfloat16).astype(jnp.float32)
    rest = value - first
    second = rest.astype(jnp.bfloat16).astype(jnp.float32)
    return first, second, rest - second


def product(left, right, left_dim, right_dim):
    l1, l2, l3 = pieces(left)
    r1, r2, r3 = pieces(right)
    lefts = jnp.concatenate([l1, l1, l2, l1, l3, l2], axis=left_dim).astype(jnp.bfloat16)
    rights = jnp.concatenate([r1, r2, r1, r3, r1, r2], axis=right_dim).astype(jnp.bfloat16)
    over = (((left_dim,), (right_dim,)), ((), ()))
    return lax.dot_general(lefts, rights, over, preferred_element_type=jnp.float32)


def factor_block(work, hooks=()):
    tiles = STRIP // 8
    sub = lax.broadcasted_iota(jnp.int32, (8, PANEL), 0)

    def spread(tile, row):
        return jnp.broadcast_to(tile[row:row + 1, :], (8, tile.shape[1]))

    def double(tile):
        return jnp.concatenate([tile, tile], axis=1)

    for base in range(0, PANEL, STRIP):
        rows = [work[base + 8 * h:base + 8 * h + 8, :] for h in range(tiles)]
        cols = {}
        for j in range(STRIP):
            for h in range(j // 8, tiles):
                cols[j, h] = jnp.broadcast_to(rows[h][:, base + j:base + j + 1], (8, PANEL))
        scale = [None] * tiles
        for k in range(0, STRIP, 2):
            own, row = divmod(k, 8)
            one = spread(cols[k, own], row)
            cross = spread(cols[k, own], row + 1)
            two = spread(cols[k + 1, own], row + 1)
            det = one * two - cross * cross
            one_inverse = 1.0 / one
            two_inverse = one / det
            ratio = cross * one_inverse
            paired = jnp.where(sub > row, det * one_inverse, one)
            scale[own] = paired if scale[own] is None else jnp.where(sub >= row, paired, scale[own])
            first, second, rest = {}, {}, {}
            for h in range(own, tiles):
                first[h] = cols[k, h] * one_inverse
                rest[h] = cols[k + 1, h] - first[h] * cross
                second[h] = rest[h] * two_inverse
                if h == own:
                    first[h] = jnp.where(sub > row, first[h], 0.0)
                    second[h] = jnp.where(sub > row + 1, second[h], 0.0)
            for j in range(k + 2, STRIP):
                peer, place = divmod(j, 8)
                entry = spread(cols[k, peer], place)
                other = spread(rest[peer], place)
                for h in range(peer, tiles):
                    cols[j, h] = cols[j, h] - first[h] * entry - second[h] * other
            line = spread(rows[own], row)
            next_line = spread(rows[own], row + 1) - double(ratio) * line
            for h in range(own, tiles):
                rows[h] = rows[h] - double(first[h]) * line - double(second[h]) * next_line
        for h in range(tiles):
            rows[h] = rows[h] * double(lax.rsqrt(scale[h]))
            work[base + 8 * h:base + 8 * h + 8, :] = rows[h]
        for hook in hooks[base // STRIP:base // STRIP + 1]:
            hook()
        low = base + STRIP
        if low < PANEL:
            strip = jnp.concatenate(rows, axis=0)
            work[low:, :] = work[low:, :] - product(strip[:, low:PANEL], strip, 0, 0)


def factor_kernel(gram, sums, rfactor, projections, square, solved, work, sems):
    order = gram.shape[0]
    lane = lax.broadcasted_iota(jnp.int32, (PANEL, PANEL), 1)
    down = lax.broadcasted_iota(jnp.int32, (PANEL, PANEL), 0)
    square[...] = gram[...]
    solved[...] = sums[...]
    copies = []
    for number, base in enumerate(range(0, order, PANEL)):
        end = base + PANEL
        work[:, :PANEL] = square[base:end, base:end]
        work[:, PANEL:] = (lane == down).astype(jnp.float32)
        factor_block(work)
        inverse = work[:, PANEL:]
        square[base:end, base:end] = jnp.where(lane >= down, work[:, :PANEL], 0.0)
        if base:
            square[base:end, :base] = jnp.zeros((PANEL, base), jnp.float32)
        answer = product(solved[:, base:end], inverse, 1, 1)
        solved[:, base:end] = answer
        if end < order:
            panel = product(inverse, square[base:end, end:], 1, 0)
            square[base:end, end:] = panel
            for top in range(end, order, PANEL):
                square[top:top + PANEL, top:] = square[top:top + PANEL, top:] - product(panel[:, top - end:top - end + PANEL], panel[:, top - end:], 0, 0)
            solved[:, end:] = solved[:, end:] - product(answer, panel, 1, 0)
        copies.append(pltpu.make_async_copy(square.at[pl.ds(base, PANEL)], rfactor.at[pl.ds(base, PANEL)], sems.at[0, number]))
        copies.append(pltpu.make_async_copy(solved.at[:, pl.ds(base, PANEL)], projections.at[:, pl.ds(base, PANEL)], sems.at[1, number]))
        copies[-2].start()
        copies[-1].start()
    for copy in copies:
        copy.wait()


def factor(gram, sums):
    vmem = pl.BlockSpec(memory_space=pltpu.VMEM)
    order = gram.shape[0]
    return pl.pallas_call(
        factor_kernel,
        out_shape=(jax.ShapeDtypeStruct(gram.shape, jnp.float32), jax.ShapeDtypeStruct(sums.shape, jnp.float32)),
        in_specs=[vmem, vmem],
        out_specs=(pl.BlockSpec(memory_space=pl.ANY),) * 2,
        scratch_shapes=[
            pltpu.VMEM(gram.shape, jnp.float32),
            pltpu.VMEM(sums.shape, jnp.float32),
            pltpu.VMEM((PANEL, 2 * PANEL), jnp.float32),
            pltpu.SemaphoreType.DMA((2, order // PANEL)),
        ],
        compiler_params=pltpu.CompilerParams(vmem_limit_bytes=16 * 1024 * 1024),
        name="factor",
    )(gram, sums)


def make_weights(seeds, weights):
    down = lax.broadcasted_iota(jnp.int32, (8, 128), 0)
    seed = jnp.broadcast_to(seeds[...], (8, 128))
    tiles = {}
    for c in range(3):
        for a in range(6):
            index = 36 * c + 6 * a + down
            first = lax.rem(seed * 7919 + index * 104729, 46337)
            second = lax.rem(first * first + seed, 46337)
            values = (second.astype(jnp.float32) / 46337.0 - 0.5) * math.sqrt(12.0 / 108.0)
            values = jnp.where(down < 6, values, 0.0)
            tiles[c, a, 0] = values
            tiles[c, a, 1] = pltpu.roll(values, 2, 0)
    none = jnp.zeros((8, 128), jnp.float32)
    for g in range(4):
        for place in range(4):
            below, right = divmod(place, 2)
            column = []
            for spot in range(32):
                half, position = divmod(spot, 16)
                c = (position - g) % 4
                a = 4 * half + ((position - c) % 16) // 4 - 2 * below
                column.append(tiles[c, a, right] if c < 3 and 0 <= a < 6 else none)
            weights[g, :, 128 * place:128 * place + 128] = jnp.concatenate(column, axis=0).astype(jnp.bfloat16)


def make_windows(images, windows):
    count, pixels = images.shape
    plane = pixels // 3
    group = lax.rem(lax.broadcasted_iota(jnp.int32, (count, BAND), 1) // 8, 4)
    for b in range(plane // BAND):
        units = [images[:, plane * c + BAND * b:plane * c + BAND * b + BAND] for c in range(3)]
        for off in range(2):
            turned = [pltpu.roll(unit, (8 * c - 4 * off) % BAND, 1) if 8 * c - 4 * off else unit for c, unit in enumerate(units)]
            for g in range(4 - off):
                mixed = jnp.where(group == (g + 1) % 4, turned[1], turned[2])
                mixed = jnp.where(group == g, turned[0], mixed)
                windows[2 * g + off, b * count:(b + 1) * count, :] = mixed


def pooled_features(count, weights, windows):
    bands = windows.shape[1] // count
    steps = bands - 1
    total = [None] * 4
    for w in range(windows.shape[0]):
        g = w // 2
        taken = jnp.concatenate([windows[w, :steps * count, :], windows[w, count:, :]], axis=1)
        for row in range(2):
            response = jnp.dot(taken, weights[g, :, 256 * row:256 * row + 256], preferred_element_type=jnp.float32)
            active = jnp.maximum(response, 0.0)
            for half in range(2):
                for p in range(2):
                    inside = [m for m in range(steps) if (2 * m + row >= 7) == (p == 1)]
                    part = sum(active[m * count:(m + 1) * count, 128 * half:128 * half + 128] for m in inside)
                    place = 2 * p + (2 * w + half >= 7)
                    total[place] = part if total[place] is None else total[place] + part
    return jnp.concatenate(total, axis=1) * (1.0 / 49.0)


def make_order(moved):
    order = moved.shape[0]
    source = lax.broadcasted_iota(jnp.int32, (order, order), 0)
    target = lax.broadcasted_iota(jnp.int32, (order, order), 1)
    moved[...] = (target == 4 * (source % 128) + source // 128).astype(jnp.float32).astype(jnp.bfloat16)


def placed_features(pooled, moved):
    count = pooled.shape[0]
    stacked = jnp.concatenate([piece.astype(jnp.bfloat16) for piece in pieces(pooled)], axis=0)
    placed = jnp.dot(stacked, moved[...], preferred_element_type=jnp.float32)
    return placed[:count] + placed[count:2 * count] + placed[2 * count:]


def feature_scratch(count, plane):
    return [
        pltpu.VMEM((4, 256, 512), jnp.bfloat16),
        pltpu.VMEM((7, plane // BAND * count, BAND), jnp.bfloat16),
        pltpu.VMEM((512, 512), jnp.bfloat16),
    ]


def features_kernel(images, seeds, block, weights, windows, moved):
    make_weights(seeds, weights)
    make_order(moved)
    make_windows(images, windows)
    block[...] = placed_features(pooled_features(images.shape[0], weights, windows), moved)


def features_block(images, seeds):
    count, pixels = images.shape
    vmem = pl.BlockSpec(memory_space=pltpu.VMEM)
    return pl.pallas_call(
        features_kernel,
        out_shape=jax.ShapeDtypeStruct((count, 4 * seeds.shape[0]), jnp.float32),
        in_specs=[vmem] * 2,
        out_specs=vmem,
        scratch_shapes=feature_scratch(count, pixels // 3),
        compiler_params=pltpu.CompilerParams(vmem_limit_bytes=24 * 1024 * 1024),
        name="features",
    )(images, seeds[None, :])


def visit(here, step, length):
    ends = jnp.minimum(here, length - 1 - here)
    near = step <= 2 * ends
    away = jnp.where(near, (step + 1) // 2, step - ends)
    below = jnp.where(near, step % 2 == 1, here > length - 1 - here)
    return jnp.where(below, here - away, here + away)


def panel_kernel(span, ridge, images, seeds, labels, square, solved, picture, seed_row, label_row, weights, windows, moved,
                 held, left_high, left_low, onehot, gram, sums, inverses, work, local_sem, send_sem, recv_sem):
    wide, deep = span
    x, z, c = lax.axis_index("sub"), lax.axis_index("img"), lax.axis_index("cls")
    across, other = wide - 1 - x, 1 - c
    count = picture.shape[0]
    order, classes = square.shape[0], solved.shape[0]
    stages = order // PANEL
    targets = [{"img": lax.rem(z + d, deep)} for d in range(1, deep)] + [{"sub": across}, {"cls": other}]
    over_x, over_c = deep - 1, deep

    loads = [pltpu.make_async_copy(seeds, seed_row, local_sem.at[0]),
             pltpu.make_async_copy(images, picture, local_sem.at[1]),
             pltpu.make_async_copy(labels, label_row, local_sem.at[2])]
    for load in loads:
        load.start()
    barrier = pltpu.get_barrier_semaphore()
    for target in targets:
        pl.semaphore_signal(barrier, inc=1, device_id=target, device_id_type=MESH)
    make_order(moved)
    square[...] = jnp.zeros_like(square)
    gram[...] = jnp.zeros_like(gram)
    sums[...] = jnp.zeros_like(sums)
    lane = lax.broadcasted_iota(jnp.int32, (PANEL, PANEL), 1)
    down = lax.broadcasted_iota(jnp.int32, (PANEL, PANEL), 0)
    for load in loads:
        load.wait()
    make_weights(seed_row, weights)
    make_windows(picture, windows)
    placed = placed_features(pooled_features(count, weights, windows), moved)
    for q in range(stages):
        held[x, z, c, 8 + PANEL * q:8 + PANEL * q + count, :] = placed[:, PANEL * q:PANEL * q + PANEL]
    held[x, z, c, 0:8, :] = jnp.broadcast_to(label_row[...].astype(jnp.float32), (8, count))
    pl.semaphore_wait(barrier, len(targets))

    def copy(way, i, j, k, q):
        low = 0 if q == 0 else 8 + PANEL * q
        slot = held.at[i, j, k, pl.ds(low, 8 + PANEL * q + count - low)]
        return pltpu.make_async_remote_copy(
            src_ref=slot, dst_ref=slot, send_sem=send_sem.at[way, i, j, q], recv_sem=recv_sem.at[i, j, k, q],
            device_id=targets[way], device_id_type=MESH)

    def start_own(q):
        for way in list(range(deep - 1)) + [over_c]:
            copy(way, x, z, c, q).start()

    def relay(q, d):
        j = visit(z, d, deep)
        copy(over_x, x, j, c, q).wait_recv()
        copy(over_x, x, j, c, q).start()
        copy(over_c, x, j, c, q).start()

    def cross(q, d):
        j = visit(z, d, deep)
        copy(over_x, across, j, c, q).wait_recv()
        copy(over_c, across, j, c, q).start()

    def accumulate(q, i, j):
        chunk = i * deep + j
        low = 8 + PANEL * q
        copy(over_c, i, j, other, q).wait_recv()
        both = jnp.concatenate([held[i, j, 0, low:low + count, :], held[i, j, 1, low:low + count, :]], axis=0)
        high = both.astype(jnp.bfloat16)
        rest = (both - high.astype(jnp.float32)).astype(jnp.bfloat16)
        left_high[chunk, PANEL * q:PANEL * q + PANEL, :] = high.T
        left_low[chunk, PANEL * q:PANEL * q + PANEL, :] = rest.T
        if q == 0:
            label = jnp.concatenate([held[i, j, 0, 0:1, :], held[i, j, 1, 0:1, :]], axis=1)
            index = lax.broadcasted_iota(jnp.int32, (classes, 2 * count), 0) + c * classes
            onehot[chunk] = (index == label.astype(jnp.int32)).astype(jnp.float32).astype(jnp.bfloat16)
        pair = jnp.concatenate([high, rest], axis=1)
        end = PANEL * q + PANEL
        top = jnp.dot(left_high[chunk, :end, :], pair, preferred_element_type=jnp.float32)
        bottom = jnp.dot(left_low[chunk, :end, :], pair, preferred_element_type=jnp.float32)
        gram[:end, PANEL * q:end] += (top[:, :PANEL] + top[:, PANEL:]) + (bottom[:, :PANEL] + bottom[:, PANEL:])
        marked = jnp.dot(onehot[chunk], pair, preferred_element_type=jnp.float32)
        sums[:, PANEL * q:end] += marked[:, :PANEL] + marked[:, PANEL:]

    copy(over_x, x, z, c, 0).start()
    for q in range(stages):
        start_own(q)

    pending = []
    for q in range(stages):
        for act in pending:
            act()
        if q == 0:
            for d in range(1, deep):
                relay(0, d)
            copy(over_x, x, z, c, 1).start()
            for d in range(deep):
                cross(0, d)

        @pl.loop(0, deep)
        def _(d):
            j = visit(z, d, deep)
            accumulate(q, x, j)
            accumulate(q, across, j)

        base, end = PANEL * q, PANEL * q + PANEL
        for i in range(q):
            rows = slice(PANEL * i, PANEL * i + PANEL)
            value = gram[rows, base:end]
            if i:
                value = value - product(square[:PANEL * i, rows], square[:PANEL * i, base:end], 0, 0)
            square[rows, base:end] = product(inverses[i], value, 1, 0)
        value = gram[base:end, base:end] + jnp.where(lane == down, ridge, 0.0)
        tail = sums[:, base:end]
        if q:
            value = value - product(square[:base, base:end], square[:base, base:end], 0, 0)
            tail = tail - product(solved[:, :base], square[:base, base:end], 1, 0)
        if q == stages - 1:
            square[base:end, base:end] = value
            solved[:, base:end] = tail
            continue
        work[:, :PANEL] = value
        work[:, PANEL:] = (lane == down).astype(jnp.float32)
        acts = []
        for d in range(deep):
            if d:
                acts.append(lambda q=q, d=d: relay(q + 1, d))
            acts.append(lambda q=q, d=d: cross(q + 1, d))
        if q + 2 < stages:
            acts.insert(deep, lambda q=q: copy(over_x, x, z, c, q + 2).start())
        strips = PANEL // STRIP

        def hook(part):
            for act in part:
                act()

        size = -(-len(acts) // strips)
        parts = [acts[n * size:n * size + size] for n in range(strips)]
        pending = []
        factor_block(work, [lambda part=part: hook(part) for part in parts])
        inverses[q] = work[:, PANEL:]
        square[base:end, base:end] = jnp.where(lane >= down, work[:, :PANEL], 0.0)
        solved[:, base:end] = product(tail, work[:, PANEL:], 1, 1)

    for q in range(stages):
        for way in range(deep - 1):
            copy(way, x, z, c, q).wait_send()

        @pl.loop(0, deep)
        def _(j):
            copy(over_x, x, j, c, q).wait_send()
            copy(over_c, x, j, c, q).wait_send()
            copy(over_c, across, j, c, q).wait_send()


def panel(images, seeds, labels, span, ridge, classes):
    count, pixels = images.shape
    order = 4 * seeds.shape[0]
    wide, deep = span
    stages = order // PANEL
    vmem, whole = pl.BlockSpec(memory_space=pltpu.VMEM), pl.BlockSpec(memory_space=pl.ANY)
    return pl.pallas_call(
        lambda *refs: panel_kernel(span, ridge, *refs),
        out_shape=(jax.ShapeDtypeStruct((order, order), jnp.float32), jax.ShapeDtypeStruct((classes, order), jnp.float32)),
        in_specs=[whole] * 3,
        out_specs=(vmem, vmem),
        scratch_shapes=[
            pltpu.VMEM((count, pixels), jnp.bfloat16),
            pltpu.VMEM((1, seeds.shape[0]), jnp.int32),
            pltpu.VMEM((1, count), jnp.int32),
            *feature_scratch(count, pixels // 3),
            pltpu.VMEM((wide, deep, 2, 8 + stages * count, PANEL), jnp.float32),
            pltpu.VMEM((wide * deep, order, 2 * count), jnp.bfloat16),
            pltpu.VMEM((wide * deep, order, 2 * count), jnp.bfloat16),
            pltpu.VMEM((wide * deep, classes, 2 * count), jnp.bfloat16),
            pltpu.VMEM((order, order), jnp.float32),
            pltpu.VMEM((classes, order), jnp.float32),
            pltpu.VMEM((stages, PANEL, PANEL), jnp.float32),
            pltpu.VMEM((PANEL, 2 * PANEL), jnp.float32),
            pltpu.SemaphoreType.DMA((3,)),
            pltpu.SemaphoreType.DMA((deep + 1, wide, deep, stages)),
            pltpu.SemaphoreType.DMA((wide, deep, 2, stages)),
        ],
        compiler_params=pltpu.CompilerParams(collective_id=0, has_side_effects=True, vmem_limit_bytes=40 * 1024 * 1024),
        name="panel",
    )(images, seeds[None, :], labels[None, :])


def finish_kernel(square, solved, rfactor, projections, block, answer, work, sems):
    order = square.shape[0]
    base = order - PANEL
    lane = lax.broadcasted_iota(jnp.int32, (PANEL, PANEL), 1)
    down = lax.broadcasted_iota(jnp.int32, (PANEL, PANEL), 0)
    copies = [pltpu.make_async_copy(square.at[pl.ds(0, base)], rfactor.at[pl.ds(0, base)], sems.at[0]),
              pltpu.make_async_copy(solved.at[:, pl.ds(0, base)], projections.at[:, pl.ds(0, base)], sems.at[1]),
              pltpu.make_async_copy(block, rfactor.at[pl.ds(base, PANEL)], sems.at[2]),
              pltpu.make_async_copy(answer, projections.at[:, pl.ds(base, PANEL)], sems.at[3])]
    copies[0].start()
    copies[1].start()
    work[:, :PANEL] = square[base:, base:]
    work[:, PANEL:] = (lane == down).astype(jnp.float32)
    factor_block(work)
    block[...] = jnp.zeros_like(block)
    block[:, base:] = jnp.where(lane >= down, work[:, :PANEL], 0.0)
    copies[2].start()
    answer[...] = product(solved[:, base:], work[:, PANEL:], 1, 1)
    copies[3].start()
    for copy in copies:
        copy.wait()


def finish(square, solved):
    vmem = pl.BlockSpec(memory_space=pltpu.VMEM)
    order = square.shape[0]
    return pl.pallas_call(
        finish_kernel,
        out_shape=(jax.ShapeDtypeStruct(square.shape, jnp.float32), jax.ShapeDtypeStruct(solved.shape, jnp.float32)),
        in_specs=[vmem, vmem],
        out_specs=(pl.BlockSpec(memory_space=pl.ANY),) * 2,
        scratch_shapes=[
            pltpu.VMEM((PANEL, order), jnp.float32),
            pltpu.VMEM((solved.shape[0], PANEL), jnp.float32),
            pltpu.VMEM((PANEL, 2 * PANEL), jnp.float32),
            pltpu.SemaphoreType.DMA((4,)),
        ],
        compiler_params=pltpu.CompilerParams(vmem_limit_bytes=16 * 1024 * 1024),
        name="finish",
    )(square, solved)


def reduced_sums(feats, labels, ridge):
    index = jnp.arange(CLASSES, dtype=jnp.int32)
    onehot = (labels[:, None] == index[None, :]).astype(jnp.float32)
    over = (((0,), (0,)), ((), ()))
    gram = lax.dot_general(feats, feats, over, precision=HIGHEST, preferred_element_type=jnp.float32)
    sums = lax.dot_general(feats, onehot, over, precision=HIGHEST, preferred_element_type=jnp.float32)
    gram = lax.psum_scatter(gram, "cls", scatter_dimension=1, tiled=True)
    sums = lax.psum_scatter(sums, "cls", scatter_dimension=1, tiled=True)
    gram, sums = lax.psum((gram, sums), ("img", "sub"))
    gram = lax.all_gather(gram, "cls", axis=1, tiled=True)
    return gram + ridge * jnp.eye(gram.shape[0], dtype=jnp.float32), sums.T


def shards(images, labels, seeds):
    count = images.shape[0]
    order = 4 * seeds.shape[0]
    span = (lax.axis_size("sub"), lax.axis_size("img"))
    pair = lax.axis_size("cls")
    ridge = RIDGE * count * span[0] * span[1] * pair
    held_bytes = span[0] * span[1] * pair * count * order * 4
    if span[0] == 2 and span[1] > 1 and pair == 2 and count == 128 and held_bytes <= GATHER_LIMIT:
        rfactor, projections = finish(*panel(images, seeds, labels, span, ridge, CLASSES // pair))
    else:
        gram, sums = reduced_sums(features_block(images, seeds), labels, ridge)
        rfactor, projections = factor(gram, sums)
    return rfactor, projections.T


def solution(mesh):
    placed = (P(("grp", "img", "sub", "cls"), None), P(("grp", "img", "sub", "cls")), P())
    return jax.shard_map(
        shards,
        mesh=mesh,
        in_specs=placed,
        out_specs=(P("grp", None), P("grp", "cls")),
        check_vma=False,
    )
```

```python
import math

import jax
import jax.numpy as jnp
from jax import lax
from jax.experimental import pallas as pl
from jax.experimental.pallas import tpu as pltpu
from jax.sharding import PartitionSpec as P

CLASSES = 1000
RIDGE = 0.001
PANEL = 128
STRIP = 32
BAND = 128
GATHER_LIMIT = 16 * 1024 * 1024
HIGHEST = lax.Precision.HIGHEST
MESH = pl.DeviceIdType.MESH


def pieces(value):
    first = value.astype(jnp.bfloat16).astype(jnp.float32)
    rest = value - first
    second = rest.astype(jnp.bfloat16).astype(jnp.float32)
    return first, second, rest - second


def product(left, right, left_dim, right_dim):
    l1, l2, l3 = pieces(left)
    r1, r2, r3 = pieces(right)
    lefts = jnp.concatenate([l1, l1, l2, l1, l3, l2], axis=left_dim).astype(jnp.bfloat16)
    rights = jnp.concatenate([r1, r2, r1, r3, r1, r2], axis=right_dim).astype(jnp.bfloat16)
    over = (((left_dim,), (right_dim,)), ((), ()))
    return lax.dot_general(lefts, rights, over, preferred_element_type=jnp.float32)


def factor_block(work, hooks=()):
    tiles = STRIP // 8
    sub = lax.broadcasted_iota(jnp.int32, (8, PANEL), 0)

    def spread(tile, row):
        return jnp.broadcast_to(tile[row:row + 1, :], (8, tile.shape[1]))

    def double(tile):
        return jnp.concatenate([tile, tile], axis=1)

    for base in range(0, PANEL, STRIP):
        rows = [work[base + 8 * h:base + 8 * h + 8, :] for h in range(tiles)]
        cols = {}
        for j in range(STRIP):
            for h in range(j // 8, tiles):
                cols[j, h] = jnp.broadcast_to(rows[h][:, base + j:base + j + 1], (8, PANEL))
        scale = [None] * tiles
        for k in range(0, STRIP, 2):
            own, row = divmod(k, 8)
            one = spread(cols[k, own], row)
            cross = spread(cols[k, own], row + 1)
            two = spread(cols[k + 1, own], row + 1)
            det = one * two - cross * cross
            one_inverse = 1.0 / one
            two_inverse = one / det
            ratio = cross * one_inverse
            paired = jnp.where(sub > row, det * one_inverse, one)
            scale[own] = paired if scale[own] is None else jnp.where(sub >= row, paired, scale[own])
            first, second, rest = {}, {}, {}
            for h in range(own, tiles):
                first[h] = cols[k, h] * one_inverse
                rest[h] = cols[k + 1, h] - first[h] * cross
                second[h] = rest[h] * two_inverse
                if h == own:
                    first[h] = jnp.where(sub > row, first[h], 0.0)
                    second[h] = jnp.where(sub > row + 1, second[h], 0.0)
            for j in range(k + 2, STRIP):
                peer, place = divmod(j, 8)
                entry = spread(cols[k, peer], place)
                other = spread(rest[peer], place)
                for h in range(peer, tiles):
                    cols[j, h] = cols[j, h] - first[h] * entry - second[h] * other
            line = spread(rows[own], row)
            next_line = spread(rows[own], row + 1) - double(ratio) * line
            for h in range(own, tiles):
                rows[h] = rows[h] - double(first[h]) * line - double(second[h]) * next_line
        for h in range(tiles):
            rows[h] = rows[h] * double(lax.rsqrt(scale[h]))
            work[base + 8 * h:base + 8 * h + 8, :] = rows[h]
        for hook in hooks[base // STRIP:base // STRIP + 1]:
            hook()
        low = base + STRIP
        if low < PANEL:
            strip = jnp.concatenate(rows, axis=0)
            work[low:, :] = work[low:, :] - product(strip[:, low:PANEL], strip, 0, 0)


def factor_kernel(gram, sums, rfactor, projections, square, solved, work, sems):
    order = gram.shape[0]
    lane = lax.broadcasted_iota(jnp.int32, (PANEL, PANEL), 1)
    down = lax.broadcasted_iota(jnp.int32, (PANEL, PANEL), 0)
    square[...] = gram[...]
    solved[...] = sums[...]
    copies = []
    for number, base in enumerate(range(0, order, PANEL)):
        end = base + PANEL
        work[:, :PANEL] = square[base:end, base:end]
        work[:, PANEL:] = (lane == down).astype(jnp.float32)
        factor_block(work)
        inverse = work[:, PANEL:]
        square[base:end, base:end] = jnp.where(lane >= down, work[:, :PANEL], 0.0)
        if base:
            square[base:end, :base] = jnp.zeros((PANEL, base), jnp.float32)
        answer = product(solved[:, base:end], inverse, 1, 1)
        solved[:, base:end] = answer
        if end < order:
            panel = product(inverse, square[base:end, end:], 1, 0)
            square[base:end, end:] = panel
            for top in range(end, order, PANEL):
                square[top:top + PANEL, top:] = square[top:top + PANEL, top:] - product(panel[:, top - end:top - end + PANEL], panel[:, top - end:], 0, 0)
            solved[:, end:] = solved[:, end:] - product(answer, panel, 1, 0)
        copies.append(pltpu.make_async_copy(square.at[pl.ds(base, PANEL)], rfactor.at[pl.ds(base, PANEL)], sems.at[0, number]))
        copies.append(pltpu.make_async_copy(solved.at[:, pl.ds(base, PANEL)], projections.at[:, pl.ds(base, PANEL)], sems.at[1, number]))
        copies[-2].start()
        copies[-1].start()
    for copy in copies:
        copy.wait()


def factor(gram, sums):
    vmem = pl.BlockSpec(memory_space=pltpu.VMEM)
    order = gram.shape[0]
    return pl.pallas_call(
        factor_kernel,
        out_shape=(jax.ShapeDtypeStruct(gram.shape, jnp.float32), jax.ShapeDtypeStruct(sums.shape, jnp.float32)),
        in_specs=[vmem, vmem],
        out_specs=(pl.BlockSpec(memory_space=pl.ANY),) * 2,
        scratch_shapes=[
            pltpu.VMEM(gram.shape, jnp.float32),
            pltpu.VMEM(sums.shape, jnp.float32),
            pltpu.VMEM((PANEL, 2 * PANEL), jnp.float32),
            pltpu.SemaphoreType.DMA((2, order // PANEL)),
        ],
        compiler_params=pltpu.CompilerParams(vmem_limit_bytes=16 * 1024 * 1024),
        name="factor",
    )(gram, sums)


def make_weights(seeds, weights):
    down = lax.broadcasted_iota(jnp.int32, (8, 128), 0)
    seed = jnp.broadcast_to(seeds[...], (8, 128))
    tiles = {}
    for c in range(3):
        for a in range(6):
            index = 36 * c + 6 * a + down
            first = lax.rem(seed * 7919 + index * 104729, 46337)
            second = lax.rem(first * first + seed, 46337)
            values = (second.astype(jnp.float32) / 46337.0 - 0.5) * math.sqrt(12.0 / 108.0)
            values = jnp.where(down < 6, values, 0.0)
            tiles[c, a, 0] = values
            tiles[c, a, 1] = pltpu.roll(values, 2, 0)
    none = jnp.zeros((8, 128), jnp.float32)
    for g in range(4):
        for place in range(4):
            below, right = divmod(place, 2)
            column = []
            for spot in range(32):
                half, position = divmod(spot, 16)
                c = (position - g) % 4
                a = 4 * half + ((position - c) % 16) // 4 - 2 * below
                column.append(tiles[c, a, right] if c < 3 and 0 <= a < 6 else none)
            weights[g, :, 128 * place:128 * place + 128] = jnp.concatenate(column, axis=0).astype(jnp.bfloat16)


def make_windows(images, windows):
    count, pixels = images.shape
    plane = pixels // 3
    group = lax.rem(lax.broadcasted_iota(jnp.int32, (count, BAND), 1) // 8, 4)
    for b in range(plane // BAND):
        units = [images[:, plane * c + BAND * b:plane * c + BAND * b + BAND] for c in range(3)]
        for off in range(2):
            turned = [pltpu.roll(unit, (8 * c - 4 * off) % BAND, 1) if 8 * c - 4 * off else unit for c, unit in enumerate(units)]
            for g in range(4 - off):
                mixed = jnp.where(group == (g + 1) % 4, turned[1], turned[2])
                mixed = jnp.where(group == g, turned[0], mixed)
                windows[2 * g + off, b * count:(b + 1) * count, :] = mixed


def pooled_features(count, weights, windows):
    bands = windows.shape[1] // count
    steps = bands - 1
    total = [None] * 4
    for w in range(windows.shape[0]):
        g = w // 2
        taken = jnp.concatenate([windows[w, :steps * count, :], windows[w, count:, :]], axis=1)
        for row in range(2):
            response = jnp.dot(taken, weights[g, :, 256 * row:256 * row + 256], preferred_element_type=jnp.float32)
            active = jnp.maximum(response, 0.0)
            for half in range(2):
                for p in range(2):
                    inside = [m for m in range(steps) if (2 * m + row >= 7) == (p == 1)]
                    part = sum(active[m * count:(m + 1) * count, 128 * half:128 * half + 128] for m in inside)
                    place = 2 * p + (2 * w + half >= 7)
                    total[place] = part if total[place] is None else total[place] + part
    return jnp.concatenate(total, axis=1) * (1.0 / 49.0)


def make_order(moved):
    order = moved.shape[0]
    source = lax.broadcasted_iota(jnp.int32, (order, order), 0)
    target = lax.broadcasted_iota(jnp.int32, (order, order), 1)
    moved[...] = (target == 4 * (source % 128) + source // 128).astype(jnp.float32).astype(jnp.bfloat16)


def placed_features(pooled, moved):
    count = pooled.shape[0]
    stacked = jnp.concatenate([piece.astype(jnp.bfloat16) for piece in pieces(pooled)], axis=0)
    placed = jnp.dot(stacked, moved[...], preferred_element_type=jnp.float32)
    return placed[:count] + placed[count:2 * count] + placed[2 * count:]


def feature_scratch(count, plane):
    return [
        pltpu.VMEM((4, 256, 512), jnp.bfloat16),
        pltpu.VMEM((7, plane // BAND * count, BAND), jnp.bfloat16),
        pltpu.VMEM((512, 512), jnp.bfloat16),
    ]


def features_kernel(images, seeds, labels, block, weights, windows, moved):
    count = images.shape[0]
    make_weights(seeds, weights)
    make_order(moved)
    make_windows(images, windows)
    block[:count, :] = placed_features(pooled_features(count, weights, windows), moved)
    block[count:, :] = jnp.zeros((8, block.shape[1]), jnp.float32)
    block[count:count + 1, :count] = labels[...].astype(jnp.float32)


def features_block(images, labels, seeds):
    count, pixels = images.shape
    vmem = pl.BlockSpec(memory_space=pltpu.VMEM)
    return pl.pallas_call(
        features_kernel,
        out_shape=jax.ShapeDtypeStruct((count + 8, 4 * seeds.shape[0]), jnp.float32),
        in_specs=[vmem] * 3,
        out_specs=vmem,
        scratch_shapes=feature_scratch(count, pixels // 3),
        compiler_params=pltpu.CompilerParams(vmem_limit_bytes=24 * 1024 * 1024),
        name="features",
    )(images, seeds[None, :], labels[None, :])


def visit(here, step, length):
    ends = jnp.minimum(here, length - 1 - here)
    near = step <= 2 * ends
    away = jnp.where(near, (step + 1) // 2, step - ends)
    below = jnp.where(near, step % 2 == 1, here > length - 1 - here)
    return jnp.where(below, here - away, here + away)


def piece_cuts(rows, deep):
    early = 8 * round(rows / (16 * (deep - 1)))
    middle = early + 8 * ((rows - early) // 16)
    return 0, early, middle, rows


def gather_kernel(span, ridge, block, gram, sums, held, local_sem, send_sem, recv_sem):
    wide, deep = span
    x, z, c = lax.axis_index("sub"), lax.axis_index("img"), lax.axis_index("cls")
    across, other = wide - 1 - x, 1 - c
    count, order = block.shape[0] - 8, block.shape[1]
    classes = sums.shape[0]
    has_up, has_down = z < deep - 1, z > 0
    targets = ({"img": z + 1}, {"img": z - 1}, {"sub": across}, {"cls": other})

    barrier = pltpu.get_barrier_semaphore()
    for exists, target in zip((has_up, has_down, True, True), targets):
        if exists is True:
            pl.semaphore_signal(barrier, inc=1, device_id=target, device_id_type=MESH)
        else:
            @pl.when(exists)
            def _():
                pl.semaphore_signal(barrier, inc=1, device_id=target, device_id_type=MESH)
    own = pltpu.make_async_copy(block, held.at[x, z, c], local_sem.at[0])
    own.start()
    gram[...] = jnp.zeros_like(gram)
    sums[...] = jnp.zeros_like(sums)
    pl.semaphore_wait(barrier, 2 + has_up.astype(jnp.int32) + has_down.astype(jnp.int32))
    own.wait()

    cuts = piece_cuts(block.shape[0], deep)

    def copy(way, i, j, k, piece):
        slot = held.at[i, j, k, pl.ds(cuts[piece], cuts[piece + 1] - cuts[piece])]
        return pltpu.make_async_remote_copy(
            src_ref=slot, dst_ref=slot, send_sem=send_sem.at[way, i, j, piece], recv_sem=recv_sem.at[i, j, k, piece],
            device_id=targets[way], device_id_type=MESH)

    def pass_along(i, j, piece):
        @pl.when(jnp.logical_and(j <= z, has_up))
        def _():
            copy(0, i, j, c, piece).start()

        @pl.when(jnp.logical_and(j >= z, has_down))
        def _():
            copy(1, i, j, c, piece).start()

    def accumulate(i, j):
        both = jnp.concatenate([held[i, j, 0, :count, :], held[i, j, 1, :count, :]], axis=0)
        high = both.astype(jnp.bfloat16)
        low = (both - high.astype(jnp.float32)).astype(jnp.bfloat16)
        high_t, low_t = high.T, low.T
        label = jnp.concatenate([held[i, j, 0, count:count + 1, :count], held[i, j, 1, count:count + 1, :count]], axis=1)
        index = lax.broadcasted_iota(jnp.int32, (classes, 2 * count), 0) + c * (CLASSES // 2)
        onehot = (index == label.astype(jnp.int32)).astype(jnp.float32).astype(jnp.bfloat16)
        for base in range(0, order, PANEL):
            rows = slice(base, base + PANEL)
            total = jnp.dot(high_t[rows], high[:, base:], preferred_element_type=jnp.float32)
            total += jnp.dot(high_t[rows], low[:, base:], preferred_element_type=jnp.float32)
            total += jnp.dot(low_t[rows], high[:, base:], preferred_element_type=jnp.float32)
            total += jnp.dot(low_t[rows], low[:, base:], preferred_element_type=jnp.float32)
            gram[rows, base:] += total
        marked = jnp.dot(onehot, high, preferred_element_type=jnp.float32)
        marked += jnp.dot(onehot, low, preferred_element_type=jnp.float32)
        sums[...] += marked

    @pl.loop(0, deep + 2)
    def _(step):
        now = visit(z, jnp.minimum(step, deep - 1), deep)
        last = visit(z, jnp.clip(step - 1, 0, deep - 1), deep)
        older = visit(z, jnp.clip(step - 2, 0, deep - 1), deep)
        arriving = step < deep
        crossing = jnp.logical_and(step >= 1, step <= deep)

        @pl.when(crossing)
        def _():
            copy(3, across, last, c, 0).wait_recv()
            pass_along(across, last, 0)
            copy(3, across, last, c, 0).start()

        def line(piece):
            @pl.when(arriving)
            def _():
                @pl.when(step > 0)
                def _():
                    copy(3, x, now, c, piece).wait_recv()

                pass_along(x, now, piece)

                @pl.when(jnp.logical_or(step == 0, piece > 0))
                def _():
                    copy(2, x, now, c, piece).start()

                copy(3, x, now, c, piece).start()

        def cross(piece):
            @pl.when(crossing)
            def _():
                copy(3, across, last, c, piece).wait_recv()
                copy(3, across, last, c, piece).start()

        def add(i, j):
            for piece in range(3):
                copy(3, i, j, other, piece).wait_recv()
            accumulate(i, j)

        line(0)
        line(1)

        @pl.when(crossing)
        def _():
            add(x, last)

        line(2)
        cross(1)

        @pl.when(step >= 2)
        def _():
            add(across, older)

        cross(2)

    for base in range(0, order, PANEL):
        rows = slice(base, base + PANEL)
        lane = lax.broadcasted_iota(jnp.int32, (PANEL, PANEL), 1)
        down = lax.broadcasted_iota(jnp.int32, (PANEL, PANEL), 0)
        gram[rows, rows] += jnp.where(lane == down, ridge, 0.0)

    @pl.loop(0, deep)
    def _(j):
        for piece in range(3):
            for i in (x, across):
                if piece == 0 or i is x:
                    @pl.when(jnp.logical_and(j <= z, has_up))
                    def _():
                        copy(0, i, j, c, piece).wait_send()

                    @pl.when(jnp.logical_and(j >= z, has_down))
                    def _():
                        copy(1, i, j, c, piece).wait_send()

                copy(3, i, j, c, piece).wait_send()

            @pl.when(jnp.logical_or(j == z, piece > 0))
            def _():
                copy(2, x, j, c, piece).wait_send()


def gathered_sums(block, span, ridge, classes):
    order = block.shape[1]
    vmem = pl.BlockSpec(memory_space=pltpu.VMEM)
    return pl.pallas_call(
        lambda *refs: gather_kernel(span, ridge, *refs),
        out_shape=(jax.ShapeDtypeStruct((order, order), jnp.float32), jax.ShapeDtypeStruct((classes, order), jnp.float32)),
        in_specs=[vmem],
        out_specs=(vmem, vmem),
        scratch_shapes=[
            pltpu.VMEM((*span, 2, *block.shape), jnp.float32),
            pltpu.SemaphoreType.DMA((1,)),
            pltpu.SemaphoreType.DMA((4, *span, 3)),
            pltpu.SemaphoreType.DMA((*span, 2, 3)),
        ],
        compiler_params=pltpu.CompilerParams(collective_id=0, has_side_effects=True, vmem_limit_bytes=32 * 1024 * 1024),
        name="gather_sums",
    )(block)


def reduced_sums(feats, labels, ridge):
    index = jnp.arange(CLASSES, dtype=jnp.int32)
    onehot = (labels[:, None] == index[None, :]).astype(jnp.float32)
    over = (((0,), (0,)), ((), ()))
    gram = lax.dot_general(feats, feats, over, precision=HIGHEST, preferred_element_type=jnp.float32)
    sums = lax.dot_general(feats, onehot, over, precision=HIGHEST, preferred_element_type=jnp.float32)
    gram = lax.psum_scatter(gram, "cls", scatter_dimension=1, tiled=True)
    sums = lax.psum_scatter(sums, "cls", scatter_dimension=1, tiled=True)
    gram, sums = lax.psum((gram, sums), ("img", "sub"))
    gram = lax.all_gather(gram, "cls", axis=1, tiled=True)
    return gram + ridge * jnp.eye(gram.shape[0], dtype=jnp.float32), sums.T


def shards(images, labels, seeds):
    count = images.shape[0]
    block = features_block(images, labels, seeds)
    order = block.shape[1]
    span = (lax.axis_size("sub"), lax.axis_size("img"))
    pair = lax.axis_size("cls")
    ridge = RIDGE * count * span[0] * span[1] * pair
    held_bytes = span[0] * span[1] * pair * block.size * 4
    if span[0] == 2 and span[1] > 1 and pair == 2 and count == 128 and held_bytes <= GATHER_LIMIT:
        gram, sums = gathered_sums(block, span, ridge, CLASSES // pair)
    else:
        gram, sums = reduced_sums(block[:count], labels, ridge)
    rfactor, projections = factor(gram, sums)
    return rfactor, projections.T


def solution(mesh):
    placed = (P(("grp", "img", "sub", "cls"), None), P(("grp", "img", "sub", "cls")), P())
    return jax.shard_map(
        shards,
        mesh=mesh,
        in_specs=placed,
        out_specs=(P("grp", None), P("grp", "cls")),
        check_vma=False,
    )
```

```python
import math

import jax
import jax.numpy as jnp
from jax import lax
from jax.experimental import pallas as pl
from jax.experimental.pallas import tpu as pltpu
from jax.sharding import PartitionSpec as P

CLASSES = 1000
RIDGE = 0.001
PANEL = 128
STRIP = 32
LEAD = 8
BAND = 128
GATHER_LIMIT = 16 * 1024 * 1024
HIGHEST = lax.Precision.HIGHEST
MESH = pl.DeviceIdType.MESH


def pieces(value):
    first = value.astype(jnp.bfloat16).astype(jnp.float32)
    rest = value - first
    second = rest.astype(jnp.bfloat16).astype(jnp.float32)
    return first, second, rest - second


def product(left, right, left_dim, right_dim):
    l1, l2, l3 = pieces(left)
    r1, r2, r3 = pieces(right)
    lefts = jnp.concatenate([l1, l1, l2, l1, l3, l2], axis=left_dim).astype(jnp.bfloat16)
    rights = jnp.concatenate([r1, r2, r1, r3, r1, r2], axis=right_dim).astype(jnp.bfloat16)
    over = (((left_dim,), (right_dim,)), ((), ()))
    return lax.dot_general(lefts, rights, over, preferred_element_type=jnp.float32)


def factor_block(work, hooks=()):
    tiles = STRIP // 8
    sub = lax.broadcasted_iota(jnp.int32, (8, PANEL), 0)

    def spread(tile, row):
        return jnp.broadcast_to(tile[row:row + 1, :], (8, tile.shape[1]))

    def double(tile):
        return jnp.concatenate([tile, tile], axis=1)

    for base in range(0, PANEL, STRIP):
        rows = [work[base + 8 * h:base + 8 * h + 8, :] for h in range(tiles)]
        cols = {}
        scale = [None] * tiles
        for k in range(0, STRIP, 2):
            for j in range(0 if k == 0 else k + LEAD, min(k + LEAD + 2, STRIP)):
                for h in range(j // 8, tiles):
                    cols[j, h] = jnp.broadcast_to(rows[h][:, base + j:base + j + 1], (8, PANEL))
            own, row = divmod(k, 8)
            one = spread(cols[k, own], row)
            cross = spread(cols[k, own], row + 1)
            two = spread(cols[k + 1, own], row + 1)
            det = one * two - cross * cross
            one_inverse = 1.0 / one
            two_inverse = one / det
            ratio = cross * one_inverse
            paired = jnp.where(sub > row, det * one_inverse, one)
            scale[own] = paired if scale[own] is None else jnp.where(sub >= row, paired, scale[own])
            first, second, rest = {}, {}, {}
            for h in range(own, tiles):
                first[h] = cols[k, h] * one_inverse
                rest[h] = cols[k + 1, h] - first[h] * cross
                second[h] = rest[h] * two_inverse
                if h == own:
                    first[h] = jnp.where(sub > row, first[h], 0.0)
                    second[h] = jnp.where(sub > row + 1, second[h], 0.0)
            for j in range(k + 2, min(k + LEAD + 2, STRIP)):
                peer, place = divmod(j, 8)
                entry = spread(cols[k, peer], place)
                other = spread(rest[peer], place)
                for h in range(peer, tiles):
                    cols[j, h] = cols[j, h] - first[h] * entry - second[h] * other
            line = spread(rows[own], row)
            next_line = spread(rows[own], row + 1) - double(ratio) * line
            for h in range(own, tiles):
                rows[h] = rows[h] - double(first[h]) * line - double(second[h]) * next_line
        for h in range(tiles):
            rows[h] = rows[h] * double(lax.rsqrt(scale[h]))
            work[base + 8 * h:base + 8 * h + 8, :] = rows[h]
        for hook in hooks[base // STRIP:base // STRIP + 1]:
            hook()
        low = base + STRIP
        if low < PANEL:
            strip = jnp.concatenate(rows, axis=0)
            work[low:, :] = work[low:, :] - product(strip[:, low:PANEL], strip, 0, 0)


def factor_kernel(gram, sums, rfactor, projections, square, solved, work, sems):
    order = gram.shape[0]
    lane = lax.broadcasted_iota(jnp.int32, (PANEL, PANEL), 1)
    down = lax.broadcasted_iota(jnp.int32, (PANEL, PANEL), 0)
    square[...] = gram[...]
    solved[...] = sums[...]
    copies = []
    for number, base in enumerate(range(0, order, PANEL)):
        end = base + PANEL
        work[:, :PANEL] = square[base:end, base:end]
        work[:, PANEL:] = (lane == down).astype(jnp.float32)
        factor_block(work)
        inverse = work[:, PANEL:]
        square[base:end, base:end] = jnp.where(lane >= down, work[:, :PANEL], 0.0)
        if base:
            square[base:end, :base] = jnp.zeros((PANEL, base), jnp.float32)
        answer = product(solved[:, base:end], inverse, 1, 1)
        solved[:, base:end] = answer
        if end < order:
            panel = product(inverse, square[base:end, end:], 1, 0)
            square[base:end, end:] = panel
            for top in range(end, order, PANEL):
                square[top:top + PANEL, top:] = square[top:top + PANEL, top:] - product(panel[:, top - end:top - end + PANEL], panel[:, top - end:], 0, 0)
            solved[:, end:] = solved[:, end:] - product(answer, panel, 1, 0)
        copies.append(pltpu.make_async_copy(square.at[pl.ds(base, PANEL)], rfactor.at[pl.ds(base, PANEL)], sems.at[0, number]))
        copies.append(pltpu.make_async_copy(solved.at[:, pl.ds(base, PANEL)], projections.at[:, pl.ds(base, PANEL)], sems.at[1, number]))
        copies[-2].start()
        copies[-1].start()
    for copy in copies:
        copy.wait()


def factor(gram, sums):
    vmem = pl.BlockSpec(memory_space=pltpu.VMEM)
    order = gram.shape[0]
    return pl.pallas_call(
        factor_kernel,
        out_shape=(jax.ShapeDtypeStruct(gram.shape, jnp.float32), jax.ShapeDtypeStruct(sums.shape, jnp.float32)),
        in_specs=[vmem, vmem],
        out_specs=(pl.BlockSpec(memory_space=pl.ANY),) * 2,
        scratch_shapes=[
            pltpu.VMEM(gram.shape, jnp.float32),
            pltpu.VMEM(sums.shape, jnp.float32),
            pltpu.VMEM((PANEL, 2 * PANEL), jnp.float32),
            pltpu.SemaphoreType.DMA((2, order // PANEL)),
        ],
        compiler_params=pltpu.CompilerParams(vmem_limit_bytes=16 * 1024 * 1024),
        name="factor",
    )(gram, sums)


def make_weights(seeds, weights):
    down = lax.broadcasted_iota(jnp.int32, (8, 128), 0)
    seed = jnp.broadcast_to(seeds[...], (8, 128))
    tiles = {}
    for c in range(3):
        for a in range(6):
            index = 36 * c + 6 * a + down
            first = lax.rem(seed * 7919 + index * 104729, 46337)
            second = lax.rem(first * first + seed, 46337)
            values = (second.astype(jnp.float32) / 46337.0 - 0.5) * math.sqrt(12.0 / 108.0)
            values = jnp.where(down < 6, values, 0.0)
            tiles[c, a, 0] = values
            tiles[c, a, 1] = pltpu.roll(values, 2, 0)
    none = jnp.zeros((8, 128), jnp.float32)
    for g in range(4):
        for place in range(4):
            below, right = divmod(place, 2)
            column = []
            for spot in range(32):
                half, position = divmod(spot, 16)
                c = (position - g) % 4
                a = 4 * half + ((position - c) % 16) // 4 - 2 * below
                column.append(tiles[c, a, right] if c < 3 and 0 <= a < 6 else none)
            weights[g, :, 128 * place:128 * place + 128] = jnp.concatenate(column, axis=0).astype(jnp.bfloat16)


def make_windows(images, windows):
    count, pixels = images.shape
    plane = pixels // 3
    group = lax.rem(lax.broadcasted_iota(jnp.int32, (count, BAND), 1) // 8, 4)
    for b in range(plane // BAND):
        units = [images[:, plane * c + BAND * b:plane * c + BAND * b + BAND] for c in range(3)]
        for off in range(2):
            turned = [pltpu.roll(unit, (8 * c - 4 * off) % BAND, 1) if 8 * c - 4 * off else unit for c, unit in enumerate(units)]
            for g in range(4 - off):
                mixed = jnp.where(group == (g + 1) % 4, turned[1], turned[2])
                mixed = jnp.where(group == g, turned[0], mixed)
                windows[2 * g + off, b * count:(b + 1) * count, :] = mixed


def pooled_features(count, weights, windows):
    bands = windows.shape[1] // count
    steps = bands - 1
    total = [None] * 4
    for w in range(windows.shape[0]):
        g = w // 2
        taken = jnp.concatenate([windows[w, :steps * count, :], windows[w, count:, :]], axis=1)
        for row in range(2):
            response = jnp.dot(taken, weights[g, :, 256 * row:256 * row + 256], preferred_element_type=jnp.float32)
            active = jnp.maximum(response, 0.0)
            for half in range(2):
                for p in range(2):
                    inside = [m for m in range(steps) if (2 * m + row >= 7) == (p == 1)]
                    part = sum(active[m * count:(m + 1) * count, 128 * half:128 * half + 128] for m in inside)
                    place = 2 * p + (2 * w + half >= 7)
                    total[place] = part if total[place] is None else total[place] + part
    return jnp.concatenate(total, axis=1) * (1.0 / 49.0)


def make_order(moved):
    order = moved.shape[0]
    source = lax.broadcasted_iota(jnp.int32, (order, order), 0)
    target = lax.broadcasted_iota(jnp.int32, (order, order), 1)
    moved[...] = (target == 4 * (source % 128) + source // 128).astype(jnp.float32).astype(jnp.bfloat16)


def placed_features(pooled, moved):
    count = pooled.shape[0]
    stacked = jnp.concatenate([piece.astype(jnp.bfloat16) for piece in pieces(pooled)], axis=0)
    placed = jnp.dot(stacked, moved[...], preferred_element_type=jnp.float32)
    return placed[:count] + placed[count:2 * count] + placed[2 * count:]


def feature_scratch(count, plane):
    return [
        pltpu.VMEM((4, 256, 512), jnp.bfloat16),
        pltpu.VMEM((7, plane // BAND * count, BAND), jnp.bfloat16),
        pltpu.VMEM((512, 512), jnp.bfloat16),
    ]


def features_kernel(images, seeds, block, weights, windows, moved):
    make_weights(seeds, weights)
    make_order(moved)
    make_windows(images, windows)
    block[...] = placed_features(pooled_features(images.shape[0], weights, windows), moved)


def features_block(images, seeds):
    count, pixels = images.shape
    vmem = pl.BlockSpec(memory_space=pltpu.VMEM)
    return pl.pallas_call(
        features_kernel,
        out_shape=jax.ShapeDtypeStruct((count, 4 * seeds.shape[0]), jnp.float32),
        in_specs=[vmem] * 2,
        out_specs=vmem,
        scratch_shapes=feature_scratch(count, pixels // 3),
        compiler_params=pltpu.CompilerParams(vmem_limit_bytes=24 * 1024 * 1024),
        name="features",
    )(images, seeds[None, :])


def visit(here, step, length):
    ends = jnp.minimum(here, length - 1 - here)
    near = step <= 2 * ends
    away = jnp.where(near, (step + 1) // 2, step - ends)
    below = jnp.where(near, step % 2 == 1, here > length - 1 - here)
    return jnp.where(below, here - away, here + away)


def piece_cuts(rows, deep):
    early = 8 * round(rows / (16 * (deep - 1)))
    middle = early + 8 * ((rows - early) // 16)
    return 0, early, middle, rows


def gather_kernel(span, ridge, images, seeds, labels, gram, sums, picture, seed_row, label_row, weights, windows, moved, held,
                  local_sem, send_sem, recv_sem):
    wide, deep = span
    x, z, c = lax.axis_index("sub"), lax.axis_index("img"), lax.axis_index("cls")
    across, other = wide - 1 - x, 1 - c
    count, order, classes = picture.shape[0], gram.shape[0], sums.shape[0]
    has_up, has_down = z < deep - 1, z > 0
    targets = ({"img": z + 1}, {"img": z - 1}, {"sub": across}, {"cls": other})

    loads = [pltpu.make_async_copy(seeds, seed_row, local_sem.at[0]),
             pltpu.make_async_copy(images, picture, local_sem.at[1]),
             pltpu.make_async_copy(labels, label_row, local_sem.at[2])]
    for load in loads:
        load.start()
    barrier = pltpu.get_barrier_semaphore()
    for exists, target in zip((has_up, has_down, True, True), targets):
        if exists is True:
            pl.semaphore_signal(barrier, inc=1, device_id=target, device_id_type=MESH)
        else:
            @pl.when(exists)
            def _():
                pl.semaphore_signal(barrier, inc=1, device_id=target, device_id_type=MESH)
    make_order(moved)
    gram[...] = jnp.zeros_like(gram)
    sums[...] = jnp.zeros_like(sums)
    loads[0].wait()
    make_weights(seed_row, weights)
    loads[1].wait()
    make_windows(picture, windows)
    held[x, z, c, :count, :] = placed_features(pooled_features(count, weights, windows), moved)
    loads[2].wait()
    held[x, z, c, count:, :] = jnp.zeros((8, order), jnp.float32)
    held[x, z, c, count:count + 1, :count] = label_row[...].astype(jnp.float32)
    pl.semaphore_wait(barrier, 2 + has_up.astype(jnp.int32) + has_down.astype(jnp.int32))

    cuts = piece_cuts(count + 8, deep)

    def copy(way, i, j, k, piece):
        slot = held.at[i, j, k, pl.ds(cuts[piece], cuts[piece + 1] - cuts[piece])]
        return pltpu.make_async_remote_copy(
            src_ref=slot, dst_ref=slot, send_sem=send_sem.at[way, i, j, piece], recv_sem=recv_sem.at[i, j, k, piece],
            device_id=targets[way], device_id_type=MESH)

    def pass_along(i, j, piece):
        @pl.when(jnp.logical_and(j <= z, has_up))
        def _():
            copy(0, i, j, c, piece).start()

        @pl.when(jnp.logical_and(j >= z, has_down))
        def _():
            copy(1, i, j, c, piece).start()

    def accumulate(i, j):
        both = jnp.concatenate([held[i, j, 0, :count, :], held[i, j, 1, :count, :]], axis=0)
        high = both.astype(jnp.bfloat16)
        low = (both - high.astype(jnp.float32)).astype(jnp.bfloat16)
        high_t, low_t = high.T, low.T
        label = jnp.concatenate([held[i, j, 0, count:count + 1, :count], held[i, j, 1, count:count + 1, :count]], axis=1)
        index = lax.broadcasted_iota(jnp.int32, (classes, 2 * count), 0) + c * (CLASSES // 2)
        onehot = (index == label.astype(jnp.int32)).astype(jnp.float32).astype(jnp.bfloat16)
        for base in range(0, order, PANEL):
            rows = slice(base, base + PANEL)
            total = jnp.dot(high_t[rows], high[:, base:], preferred_element_type=jnp.float32)
            total += jnp.dot(high_t[rows], low[:, base:], preferred_element_type=jnp.float32)
            total += jnp.dot(low_t[rows], high[:, base:], preferred_element_type=jnp.float32)
            total += jnp.dot(low_t[rows], low[:, base:], preferred_element_type=jnp.float32)
            gram[rows, base:] += total
        marked = jnp.dot(onehot, high, preferred_element_type=jnp.float32)
        marked += jnp.dot(onehot, low, preferred_element_type=jnp.float32)
        sums[...] += marked

    @pl.loop(0, deep + 2)
    def _(step):
        now = visit(z, jnp.minimum(step, deep - 1), deep)
        last = visit(z, jnp.clip(step - 1, 0, deep - 1), deep)
        older = visit(z, jnp.clip(step - 2, 0, deep - 1), deep)
        arriving = step < deep
        crossing = jnp.logical_and(step >= 1, step <= deep)

        @pl.when(crossing)
        def _():
            copy(3, across, last, c, 0).wait_recv()
            pass_along(across, last, 0)
            copy(3, across, last, c, 0).start()

        def line(piece):
            @pl.when(arriving)
            def _():
                @pl.when(step > 0)
                def _():
                    copy(3, x, now, c, piece).wait_recv()

                pass_along(x, now, piece)

                @pl.when(jnp.logical_or(step == 0, piece > 0))
                def _():
                    copy(2, x, now, c, piece).start()

                copy(3, x, now, c, piece).start()

        def cross(piece):
            @pl.when(crossing)
            def _():
                copy(3, across, last, c, piece).wait_recv()
                copy(3, across, last, c, piece).start()

        def add(i, j):
            for piece in range(3):
                copy(3, i, j, other, piece).wait_recv()
            accumulate(i, j)

        line(0)
        line(1)

        @pl.when(crossing)
        def _():
            add(x, last)

        line(2)
        cross(1)

        @pl.when(step >= 2)
        def _():
            add(across, older)

        cross(2)

    for base in range(0, order, PANEL):
        rows = slice(base, base + PANEL)
        lane = lax.broadcasted_iota(jnp.int32, (PANEL, PANEL), 1)
        down = lax.broadcasted_iota(jnp.int32, (PANEL, PANEL), 0)
        gram[rows, rows] += jnp.where(lane == down, ridge, 0.0)

    @pl.loop(0, deep)
    def _(j):
        for piece in range(3):
            for i in (x, across):
                if piece == 0 or i is x:
                    @pl.when(jnp.logical_and(j <= z, has_up))
                    def _():
                        copy(0, i, j, c, piece).wait_send()

                    @pl.when(jnp.logical_and(j >= z, has_down))
                    def _():
                        copy(1, i, j, c, piece).wait_send()

                copy(3, i, j, c, piece).wait_send()

            @pl.when(jnp.logical_or(j == z, piece > 0))
            def _():
                copy(2, x, j, c, piece).wait_send()


def gathered_sums(images, seeds, labels, span, ridge, classes):
    count, pixels = images.shape
    order = 4 * seeds.shape[0]
    vmem, far = pl.BlockSpec(memory_space=pltpu.VMEM), pl.BlockSpec(memory_space=pltpu.MemorySpace.HBM)
    return pl.pallas_call(
        lambda *refs: gather_kernel(span, ridge, *refs),
        out_shape=(jax.ShapeDtypeStruct((order, order), jnp.float32), jax.ShapeDtypeStruct((classes, order), jnp.float32)),
        in_specs=[far] * 3,
        out_specs=(vmem, vmem),
        scratch_shapes=[
            pltpu.VMEM((count, pixels), jnp.bfloat16),
            pltpu.VMEM((1, seeds.shape[0]), jnp.int32),
            pltpu.VMEM((1, count), jnp.int32),
            *feature_scratch(count, pixels // 3),
            pltpu.VMEM((*span, 2, count + 8, order), jnp.float32),
            pltpu.SemaphoreType.DMA((3,)),
            pltpu.SemaphoreType.DMA((4, *span, 3)),
            pltpu.SemaphoreType.DMA((*span, 2, 3)),
        ],
        compiler_params=pltpu.CompilerParams(collective_id=0, has_side_effects=True, vmem_limit_bytes=32 * 1024 * 1024),
        name="gather_sums",
    )(*(pltpu.with_memory_space_constraint(v, pltpu.MemorySpace.HBM) for v in (images, seeds[None, :], labels[None, :])))


def reduced_sums(feats, labels, ridge):
    index = jnp.arange(CLASSES, dtype=jnp.int32)
    onehot = (labels[:, None] == index[None, :]).astype(jnp.float32)
    over = (((0,), (0,)), ((), ()))
    gram = lax.dot_general(feats, feats, over, precision=HIGHEST, preferred_element_type=jnp.float32)
    sums = lax.dot_general(feats, onehot, over, precision=HIGHEST, preferred_element_type=jnp.float32)
    gram = lax.psum_scatter(gram, "cls", scatter_dimension=1, tiled=True)
    sums = lax.psum_scatter(sums, "cls", scatter_dimension=1, tiled=True)
    gram, sums = lax.psum((gram, sums), ("img", "sub"))
    gram = lax.all_gather(gram, "cls", axis=1, tiled=True)
    return gram + ridge * jnp.eye(gram.shape[0], dtype=jnp.float32), sums.T


def shards(images, labels, seeds):
    count = images.shape[0]
    span = (lax.axis_size("sub"), lax.axis_size("img"))
    pair = lax.axis_size("cls")
    ridge = RIDGE * count * span[0] * span[1] * pair
    held_bytes = span[0] * span[1] * pair * (count + 8) * 16 * seeds.shape[0]
    if span[0] == 2 and span[1] > 1 and pair == 2 and count == 128 and held_bytes <= GATHER_LIMIT:
        gram, sums = gathered_sums(images, seeds, labels, span, ridge, CLASSES // pair)
    else:
        gram, sums = reduced_sums(features_block(images, seeds), labels, ridge)
    rfactor, projections = factor(gram, sums)
    return rfactor, projections.T


def solution(mesh):
    placed = (P(("grp", "img", "sub", "cls"), None), P(("grp", "img", "sub", "cls")), P())
    return jax.shard_map(
        shards,
        mesh=mesh,
        in_specs=placed,
        out_specs=(P("grp", None), P("grp", "cls")),
        check_vma=False,
    )
```
